128 devices in a mesh: tm: 32 (over z, y, core), rows: 4 (over x).
Axes of the slice: x: 4, y: 4, z: 4, core: 2. Of those that a mesh axis runs over, the one named last changes fastest.
Arguments:
- covars: bfloat16 [524288, 128], P(('tm', 'rows')), may hold values from -5 to 5
- strata: int32 [524288], P(('tm', 'rows')), may hold values from 0 to 511
- centers: int32 [524288], P(('tm', 'rows')), may hold values from 0 to 2047
- events: int32 [524288], P(('tm', 'rows')), may hold values 0 or 1
- counts: int32 [128], P(('tm', 'rows')), may hold values from 1024 to 4096, as said below
- beta: float32 [128], replicated, may hold values from -0.4 to 0.4
- frailty: float32 [2048], replicated, may hold values from -3 to 3
Outputs:
- score: float32 [128], replicated
- info: float32 [128, 128], replicated
- center_score: float32 [2048], P(('tm', 'rows'))
- center_info: float32 [2048], P(('tm', 'rows'))
- center_cross: float32 [2048, 128], P(('tm', 'rows'))
The draws below stay inside these ranges and needn't reach their ends.
Inputs may be any that keep to these rules, and one draw needn't show every extreme that they name: `counts`: each shard's live records come first; some shard is full.
All inputs are finite; a program needn't handle non-finite values. No bound on the sum of `events` on one device may be relied on, other than what follows from the above.
Results may differ from the reference program's by a relative error of at most 0.00067.
Values sent between devices are 32-bit elements; how exact they have to be, the bound alone decides.
No kernel may reach another device: no remote copies, remote signals or barrier semaphores. Data moves between devices by JAX's collectives and lax.ppermute only.
A program may use at most 64 MiB of HBM per device.

```python
import math
import jax
import jax.numpy as jnp
import numpy as np
from jax import lax

P_SIZE = 128
STRATA = 512
REC_DEV = 4096
CENTERS_DEV = 16
SHARDS = 128
RECORDS = 524288
CENTERS = 2048


def draw_covars(key, part):
    shift_key = jax.random.fold_in(key, 11)
    noise_key = jax.random.fold_in(key, 12)
    shift = jax.random.uniform(shift_key, (P_SIZE,), jnp.float32, -1.0, 1.0)
    noise = jnp.clip(jax.random.normal(noise_key, (RECORDS, P_SIZE), jnp.float32), -4.0, 4.0)
    return (noise + shift[None, :]).astype(jnp.bfloat16)


def draw_counts(key, part):
    value_key = jax.random.fold_in(key, 21)
    pick_key = jax.random.fold_in(key, 22)
    values = jax.random.randint(value_key, (SHARDS,), REC_DEV // 4, REC_DEV + 1)
    chosen = jax.random.randint(pick_key, (), 0, SHARDS)
    return values.at[chosen].set(REC_DEV)


def set_ends(array, own_key, smallest, top_value):
    index_at = [jax.random.randint(jax.random.fold_in(own_key, axis), (), 0, length) for axis, length in enumerate(array.shape)]
    widest = array.shape.index(max(array.shape))
    neighbour = index_at[:widest] + [(index_at[widest] + 1) % array.shape[widest]] + index_at[widest + 1:]
    return array.at[tuple(index_at)].set(smallest).at[tuple(neighbour)].set(top_value)


def rank_table(amount, slope):
    weights = [(1 << 20) // math.isqrt(rank ** slope) + 1 for rank in range(1, amount + 1)]
    deviation = 1 + sum(weights) // (1 << 30)
    return np.cumsum(np.array([max(1, weight // deviation) for weight in weights]))


def skewed_ids(key, dims, count, lean):
    grid = rank_table(count, lean)
    ticket = jax.random.randint(jax.random.fold_in(key, 1), dims, 0, int(grid[count - 1]))
    grade = jnp.searchsorted(jnp.asarray(grid, jnp.int32), ticket, side="right")
    return jax.random.permutation(jax.random.fold_in(key, 2), count)[grade].astype(jnp.int32)


def gaussian(key, dims, width, limit, held_as=jnp.bfloat16):
    entries = jax.random.normal(key, dims, jnp.float32) * width
    return jnp.minimum(jnp.maximum(entries, -limit), limit).astype(held_as)


def setup_inputs(seed: int = 0) -> dict:
    key_of = jax.random.split(jax.random.key(seed), 8)
    covars = draw_covars(jax.random.fold_in(key_of[7], 71), 0)
    strata = set_ends(jax.random.randint(key_of[1], (RECORDS,), 0, STRATA), jax.random.fold_in(key_of[1], 1), 0, STRATA - 1).astype(jnp.int32)
    centers = set_ends(skewed_ids(key_of[2], (RECORDS,), CENTERS, 1), jax.random.fold_in(key_of[2], 3), 0, CENTERS - 1).astype(jnp.int32)
    events = set_ends((jax.random.randint(key_of[3], (RECORDS,), 0, 2) < 1).astype(jnp.int32), jax.random.fold_in(key_of[3], 1), 0, 1)
    counts = draw_counts(jax.random.fold_in(key_of[7], 71), 0)
    beta = gaussian(key_of[5], (P_SIZE,), 0.08, 0.4, jnp.float32)
    frailty = gaussian(key_of[6], (CENTERS,), 0.6, 3.0, jnp.float32)
    return dict(covars=covars, strata=strata, centers=centers, events=events, counts=counts, beta=beta, frailty=frailty)


def block_suffix(group_ids, weights, weighted, groups):
    record_count = group_ids.shape[0]
    block_size = min(512, record_count)
    blocks = record_count // block_size
    positions = jnp.arange(block_size)
    upper = positions[None, :] >= positions[:, None]
    labels = jnp.arange(groups)

    def advance(carry, item):
        carry_zero, carry_one = carry
        block_ids, block_weights, block_rows = item
        shared = (block_ids[:, None] == block_ids[None, :]) & upper
        local_one = jnp.dot(shared.astype(jnp.float32), block_rows.astype(jnp.float32), precision=lax.Precision.HIGHEST)
        local_zero = jnp.dot(shared.astype(jnp.float32), block_weights, precision=lax.Precision.HIGHEST)
        result = (local_zero + carry_zero[block_ids], local_one + carry_one[block_ids])
        member = (block_ids[:, None] == labels[None, :]).astype(jnp.float32)
        carry_one = carry_one + jnp.dot(member.T, block_rows.astype(jnp.float32), precision=lax.Precision.HIGHEST)
        carry_zero = carry_zero + jnp.dot(block_weights, member, precision=lax.Precision.HIGHEST)
        return ((carry_zero, carry_one), result)
    init = (jnp.zeros((groups,), jnp.float32), jnp.zeros((groups, weighted.shape[1]), jnp.float32))
    items = (group_ids.reshape(blocks, block_size), weights.reshape(blocks, block_size), weighted.reshape(blocks, block_size, weighted.shape[1]))
    final, outputs = lax.scan(advance, init, items, reverse=True)
    return (outputs[0].reshape(record_count), outputs[1].reshape(record_count, weighted.shape[1]))

def block_prefix(group_ids, increments, groups):
    record_count = group_ids.shape[0]
    block_size = min(512, record_count)
    blocks = record_count // block_size
    positions = jnp.arange(block_size)
    lower = positions[None, :] <= positions[:, None]
    labels = jnp.arange(groups)

    def advance(carry, item):
        block_ids, block_incr = item
        shared = ((block_ids[:, None] == block_ids[None, :]) & lower).astype(jnp.float32)
        result = jnp.dot(shared, block_incr, precision=lax.Precision.HIGHEST) + carry[block_ids]
        member = (block_ids[:, None] == labels[None, :]).astype(jnp.float32)
        return (carry + jnp.dot(block_incr, member, precision=lax.Precision.HIGHEST), result)
    final, outputs = lax.scan(advance, jnp.zeros((groups,), jnp.float32), (group_ids.reshape(blocks, block_size), increments.reshape(blocks, block_size)))
    return outputs.reshape(record_count)

def reference(covars, strata, centers, events, counts, beta, frailty):
    total = covars.shape[0]
    record_index = jnp.arange(total)
    live = record_index % REC_DEV < counts[record_index // REC_DEV]
    dense = covars.astype(jnp.float32)
    eta = jnp.dot(dense, beta, precision=lax.Precision.HIGHEST) + frailty[centers]
    weights = jnp.where(live, jnp.exp(eta), 0.0)
    weighted = (weights[:, None] * dense).astype(jnp.bfloat16)
    suffix_zero, suffix_one = block_suffix(strata, weights, weighted, STRATA)
    flags = jnp.where(live, events, 0).astype(jnp.float32)
    safe_zero = jnp.where(flags > 0, suffix_zero, 1.0)
    increments = jnp.where(flags > 0, flags / safe_zero, 0.0)
    hazard = block_prefix(strata, increments, STRATA)
    exposure = weights * hazard
    mean_rows = jnp.where(flags[:, None] > 0, suffix_one / safe_zero[:, None], 0.0)
    mean_low = mean_rows.astype(jnp.bfloat16)
    loaded = (exposure[:, None] * dense).astype(jnp.bfloat16)
    gradient = jnp.dot(flags, dense, precision=lax.Precision.HIGHEST) - lax.optimization_barrier(jnp.sum(mean_rows, axis=0))
    curvature = jnp.dot(dense.T, loaded.astype(jnp.float32), precision=lax.Precision.HIGHEST) - jnp.dot(mean_low.T, mean_low, preferred_element_type=jnp.float32)
    score = gradient / math.sqrt(RECORDS)
    info = curvature / RECORDS
    load = REC_DEV // CENTERS_DEV
    root = math.sqrt(load)
    center_score = jax.ops.segment_sum(flags - exposure, centers, num_segments=CENTERS) / root - 0.5 * frailty
    center_info = jax.ops.segment_sum(exposure, centers, num_segments=CENTERS) / load + 0.5
    center_cross = jax.ops.segment_sum(loaded.astype(jnp.float32), centers, num_segments=CENTERS) / root
    return (score, info, center_score, center_info, center_cross)
```

```python
import math

import jax
import jax.numpy as jnp
from jax import lax
from jax.experimental import pallas as pl
from jax.experimental.pallas import tpu as pltpu
from jax.sharding import PartitionSpec as P

STRATA = 512
CENTERS_DEV = 16
AXES = ("tm", "rows")
BLOCK = 512
LANES = 128
F32 = jnp.float32
BF16 = jnp.bfloat16
NN = (((1,), (0,)), ((), ()))
NT = (((1,), (1,)), ((), ()))
TN = (((0,), (0,)), ((), ()))


def mxu(left, right, dims=NN):
    return lax.dot_general(left, right, dims, preferred_element_type=F32)


def iota(shape, dim):
    return lax.broadcasted_iota(jnp.int32, shape, dim)


def split3(value):
    high = value.astype(BF16).astype(F32)
    rest = value - high
    middle = rest.astype(BF16).astype(F32)
    return high, middle, (rest - middle).astype(BF16).astype(F32)


def stack(rows, height):
    at = iota((height, rows[0].shape[1]), 0)
    out = jnp.zeros(at.shape, F32)
    for place, row in enumerate(rows):
        out = jnp.where(at == place, row, out)
    return out.astype(BF16)


def one_hot(ids, height):
    return jnp.where(iota((height, ids.shape[1]), 0) == ids, 1.0, 0.0).astype(BF16)


def columns(rows, width=LANES):
    return mxu(stack(rows, 8), jnp.ones((8, width), BF16), TN)


def table_rows(table):
    return jnp.concatenate(split3(table), axis=0).astype(BF16)


def look_up(rows, upper, lower_hot, height):
    picked = mxu(rows, lower_hot)
    picked = picked[:height] + picked[height : 2 * height] + picked[2 * height :]
    hit = iota(picked.shape, 0) == upper
    return jnp.sum(jnp.where(hit, picked, 0.0), axis=0, keepdims=True)


def add_up(values, upper, lower_hot, height):
    at = iota((height, values.shape[1]), 0)
    parts = [jnp.where(at == upper, part, 0.0) for part in split3(values)]
    sums = mxu(jnp.concatenate(parts, axis=0).astype(BF16), lower_hot, NT)
    return sums[:height] + sums[height : 2 * height] + sums[2 * height :]


def id_columns(ids):
    upper = ids & ~255
    column = columns([upper.astype(F32), (ids - upper).astype(F32)])
    return jnp.concatenate([column] * (STRATA // LANES), axis=1)


def same_and_later(ids, id_column):
    square = (BLOCK, BLOCK)
    later = iota(square, 1) >= iota(square, 0)
    return jnp.where((id_column == ids.astype(F32)) & later, 1.0, 0.0).astype(BF16)


def members(id_column):
    labels = iota((BLOCK, STRATA), 1).astype(F32)
    return jnp.where(id_column == labels, 1.0, 0.0).astype(BF16)


def strided(start, count):
    return pl.ds(start, count, stride=8)


def weigh_kernel(counts, strata, centers, covars, beta, frailty, w_out, wx_out, send):
    records = covars.shape[0]
    betas = stack(split3(beta[...]), 8)
    table = table_rows(frailty[...])
    total_zero = jnp.zeros((8, LANES), F32)
    total_one = jnp.zeros((STRATA, LANES), F32)
    for start in range(0, records, BLOCK):
        span = pl.ds(start, BLOCK)
        ids, owners, rows = strata[:, span], centers[:, span], covars[span, :]
        eta = jnp.sum(mxu(betas, rows, NT), axis=0, keepdims=True) + look_up(
            table, owners >> 7, one_hot(owners & 127, LANES), frailty.shape[0]
        )
        live = iota((1, BLOCK), 1) + start < counts[0]
        weight = jnp.where(live, jnp.exp(eta), 0.0)
        w_out[:, span] = weight
        weighted = (columns(split3(weight)) * rows.astype(F32)).astype(BF16)
        wx_out[span, :] = weighted
        total_one = total_one + mxu(one_hot(ids, STRATA), weighted)
        total_zero = total_zero + add_up(weight, ids >> 7, one_hot(ids & 127, LANES), 8)
    devices = send.shape[0] // 8
    for place in range(4):
        send[strided(place, devices), :] = jnp.broadcast_to(
            total_zero[place : place + 1], (devices, LANES)
        )
        send[strided(4 + place, devices), :] = total_one[place * LANES : (place + 1) * LANES]


def suffix_kernel(strata, w_in, wx_in, zero_out, one_out):
    records = wx_in.shape[0]
    carry_zero = jnp.zeros((8, LANES), F32)
    carry_one = jnp.zeros((STRATA, LANES), F32)
    for start in reversed(range(0, records, BLOCK)):
        span = pl.ds(start, BLOCK)
        ids, weight, weighted = strata[:, span], w_in[:, span], wx_in[span, :]
        id_column = id_columns(ids)
        shared = same_and_later(ids, id_column)
        lower_hot = one_hot(ids & 127, LANES)
        zero = jnp.sum(mxu(stack(split3(weight), 8), shared, NT), axis=0, keepdims=True)
        zero_out[:, span] = zero + look_up(table_rows(carry_zero), ids >> 7, lower_hot, 8)
        high = carry_one.astype(BF16)
        low = (carry_one - high.astype(F32)).astype(BF16)
        later = mxu(members(id_column), jnp.concatenate([high, low], axis=1))
        one_out[span, :] = mxu(shared, weighted) + later[:, :LANES] + later[:, LANES:]
        carry_one = carry_one + mxu(one_hot(ids, STRATA), weighted)
        carry_zero = carry_zero + add_up(weight, ids >> 7, lower_hot, 8)


def hazard_kernel(counts, mine, strata, events, zero_in, received, q_out, send, later):
    records = strata.shape[1]
    devices = received.shape[0] // 8
    running = jnp.zeros((8, LANES), F32)
    for device in reversed(range(devices)):
        slab = pl.ds(device * 8, 8)
        later[slab, :] = running
        running = running + received[slab, :]
    table = table_rows(later[pl.ds(pl.multiple_of(mine[0] * 8, 8), 8), :])
    total = jnp.zeros((8, LANES), F32)
    for start in range(0, records, BLOCK):
        span = pl.ds(start, BLOCK)
        ids = strata[:, span]
        lower_hot = one_hot(ids & 127, LANES)
        zero = zero_in[:, span] + look_up(table, ids >> 7, lower_hot, 8)
        live = iota((1, BLOCK), 1) + start < counts[0]
        happened = live & (events[:, span] > 0)
        increment = jnp.where(happened, 1.0 / jnp.where(happened, zero, 1.0), 0.0)
        q_out[:, span] = increment
        total = total + add_up(increment, ids >> 7, lower_hot, 8)
    mask = iota((8, LANES), 0) < 4
    for device in range(devices):
        slab = pl.ds(device * 8, 8)
        send[slab, :] = jnp.where(mask, total, later[slab, :])


def prefix_kernel(strata, q_in, out):
    records = strata.shape[1]
    carry = jnp.zeros((8, LANES), F32)
    for start in range(0, records, BLOCK):
        span = pl.ds(start, BLOCK)
        ids, increment = strata[:, span], q_in[:, span]
        shared = same_and_later(ids, id_columns(ids))
        lower_hot = one_hot(ids & 127, LANES)
        local = jnp.sum(mxu(stack(split3(increment), 8), shared), axis=0, keepdims=True)
        out[:, span] = local + look_up(table_rows(carry), ids >> 7, lower_hot, 8)
        carry = carry + add_up(increment, ids >> 7, lower_hot, 8)


def moments_kernel(
    counts, mine, strata, centers, events, w_in, q_in, hazard_in, covars, one_in, received,
    loaded_out, pack,
):
    records, width = covars.shape
    devices = received.shape[0] // 8
    before = (iota((devices * 8, LANES), 0) >> 3) < mine[0]
    earlier = jnp.where(before, received[...], 0.0).reshape(devices, 8, LANES).sum(axis=0)
    table = table_rows(earlier)
    later = jnp.concatenate([received[strided(4 + r, devices), :] for r in range(4)], axis=0)
    high = later.astype(BF16)
    low = (later - high.astype(F32)).astype(BF16)
    later = jnp.concatenate([high, low], axis=1)
    sixteen = iota((16, 2 * LANES), 0)
    left = iota((16, 2 * LANES), 1) < LANES
    spread = jnp.where(
        (left & (sixteen < 3)) | (~left & (sixteen >= 3) & (sixteen < 6)), 1.0, 0.0
    ).astype(BF16)
    groups = 16
    pairs = jnp.zeros((4 * groups, LANES), F32)
    curvature = jnp.zeros((width, width), F32)
    gradient = jnp.zeros((1, width), F32)
    for start in range(0, records, BLOCK):
        span = pl.ds(start, BLOCK)
        ids, owners, rows = strata[:, span], centers[:, span], covars[span, :]
        increment = q_in[:, span]
        hazard = hazard_in[:, span] + look_up(table, ids >> 7, one_hot(ids & 127, LANES), 8)
        exposure = w_in[:, span] * hazard
        live = iota((1, BLOCK), 1) + start < counts[0]
        happened = jnp.where(live & (events[:, span] > 0), 1.0, 0.0)
        parts = split3(exposure)
        both = mxu(stack([*parts, *split3(increment)], 16), spread, TN)
        loaded = (both[:, :LANES] * rows.astype(F32)).astype(BF16)
        loaded_out[span, :] = loaded
        outside = mxu(members(id_columns(ids)), later)
        mean = (one_in[span, :] + outside[:, :LANES] + outside[:, LANES:]) * both[:, LANES:]
        mean_low = mean.astype(BF16)
        curvature = curvature + mxu(rows, loaded, TN) - mxu(mean_low, mean_low, TN)
        flags = mxu(stack([happened], 8), rows)
        gradient = gradient + flags[:1] - jnp.sum(mean, axis=0, keepdims=True)
        at = iota((groups, BLOCK), 0)
        chosen = [jnp.where(at == owners >> 7, part, 0.0) for part in (*parts, happened)]
        pairs = pairs + mxu(
            jnp.concatenate(chosen, axis=0).astype(BF16), one_hot(owners & 127, LANES), NT
        )
    exposed = pairs[:groups] + pairs[groups : 2 * groups] + pairs[2 * groups : 3 * groups]
    pack[0:width, :] = curvature
    pack[width : width + 8, :] = jnp.broadcast_to(gradient, (8, width))
    pack[width + 8 : width + 24, :] = pairs[3 * groups :] - exposed
    pack[width + 24 : width + 40, :] = exposed


def cross_kernel(centers, loaded, out):
    tile = 256
    for start in range(0, out.shape[0], tile):
        out[pl.ds(start, tile), :] = mxu(one_hot(centers[...] - start, tile), loaded[...])


def call(kernel, out_shape, scratch=(), scalars=0, **kwargs):
    def run(*args):
        specs = [
            pl.BlockSpec(memory_space=pltpu.SMEM if place < scalars else pltpu.VMEM)
            for place in range(len(args))
        ]
        return pl.pallas_call(
            kernel,
            out_shape=out_shape,
            in_specs=specs,
            out_specs=jax.tree.map(lambda _: pl.BlockSpec(memory_space=pltpu.VMEM), out_shape),
            scratch_shapes=list(scratch),
            name=kernel.__name__,
            **kwargs,
        )(*args)

    return run


def shaped(*shape, dtype=F32):
    return jax.ShapeDtypeStruct(shape, dtype)


def place_of(z, y, c, x):
    return ((z * 4 + y) * 2 + c) * 4 + x


def moves(step):
    grid = [
        (z, y, c, x) for z in range(4) for y in range(4) for c in range(2) for x in range(4)
    ]
    return [(place_of(*at), place_of(*step(*at))) for at in grid]


def sum_everywhere(value):
    value = value + lax.ppermute(value, AXES, moves(lambda z, y, c, x: (z, y, 1 - c, x)))
    rings = (
        lambda k: lambda z, y, c, x: (z, y, c, (x + k) % 4),
        lambda k: lambda z, y, c, x: (z, (y + k) % 4, c, x),
        lambda k: lambda z, y, c, x: ((z + k) % 4, y, c, x),
    )
    for ring in rings:
        others = [lax.ppermute(value, AXES, moves(ring(k))) for k in (1, 2, 3)]
        value = (value + others[1]) + (others[0] + others[2])
    return value


def exchange(value):
    devices = value.shape[0] // 8
    out = lax.all_to_all(value.reshape(devices, 8, LANES), AXES, 0, 0, tiled=True)
    return out.reshape(devices * 8, LANES)


def body(covars, strata, centers, events, counts, beta, frailty):
    records, width = covars.shape
    devices = lax.axis_size("tm") * lax.axis_size("rows")
    center_total = CENTERS_DEV * devices
    mine = lax.axis_index(AXES)
    me = mine.reshape(1).astype(jnp.int32)
    strata, centers, events = (part.reshape(1, records) for part in (strata, centers, events))
    slabs = shaped(devices * 8, LANES)
    line = shaped(1, records)
    weights, weighted, totals = call(
        weigh_kernel, (line, shaped(records, width, dtype=BF16), slabs), scalars=1
    )(counts, strata, centers, covars, beta.reshape(1, width), frailty.reshape(-1, LANES))
    received = exchange(totals)
    suffix_zero, suffix_one = call(suffix_kernel, (line, shaped(records, width)))(
        strata, weights, weighted
    )
    increments, send = call(
        hazard_kernel, (line, slabs), scratch=[pltpu.VMEM((devices * 8, LANES), F32)], scalars=2
    )(counts, me, strata, events, suffix_zero, received)
    arrived = exchange(send)
    local_hazard = call(prefix_kernel, line)(strata, increments)
    loaded, pack = call(
        moments_kernel,
        (shaped(records, width, dtype=BF16), shaped(width + 40, LANES)),
        scalars=2,
    )(
        counts, me, strata, centers, events, weights, increments, local_hazard, covars,
        suffix_one, arrived,
    )
    cross = call(cross_kernel, shaped(center_total, width))(centers, loaded)
    shares = lax.all_to_all(
        cross.reshape(devices, CENTERS_DEV, width), AXES, 0, 0, tiled=True
    )
    pack = sum_everywhere(pack)
    total = records * devices
    info = pack[:width] / total
    score = pack[width] / math.sqrt(total)
    load = records // CENTERS_DEV
    root = math.sqrt(load)
    pairs = pack[width + 8 :].reshape(2, center_total)
    first = mine * CENTERS_DEV
    pairs = lax.dynamic_slice_in_dim(pairs, first, CENTERS_DEV, axis=1)
    frailty_mine = lax.dynamic_slice_in_dim(frailty, first, CENTERS_DEV)
    center_score = pairs[0] / root - 0.5 * frailty_mine
    center_info = pairs[1] / load + 0.5
    center_cross = jnp.sum(shares, axis=0) / root
    return (score, info, center_score, center_info, center_cross)


def solution(mesh):
    in_specs = (
        P(AXES, None),
        P(AXES),
        P(AXES),
        P(AXES),
        P(AXES),
        P(),
        P(),
    )
    out_specs = (P(), P(), P(AXES), P(AXES), P(AXES, None))
    return jax.shard_map(body, mesh=mesh, in_specs=in_specs, out_specs=out_specs, check_vma=False)
```

```python
import functools
import math

import jax
import jax.numpy as jnp
from jax import lax
from jax.experimental import pallas as pl
from jax.experimental.pallas import tpu as pltpu
from jax.sharding import Mesh
from jax.sharding import PartitionSpec as P


STRATA = 512
CENTERS_DEV = 16
AXES = ("z", "y", "core", "x")
CHIPS = ("z", "y", "x")
BLOCK = 512
LANES = 128
F32 = jnp.float32
BF16 = jnp.bfloat16
NN = (((1,), (0,)), ((), ()))
NT = (((1,), (1,)), ((), ()))
TN = (((0,), (0,)), ((), ()))


def mxu(left, right, dims=NN):
    return lax.dot_general(left, right, dims, preferred_element_type=F32)


def iota(shape, dim):
    return lax.broadcasted_iota(jnp.int32, shape, dim)


def split3(value):
    high = value.astype(BF16).astype(F32)
    rest = value - high
    middle = rest.astype(BF16).astype(F32)
    return high, middle, (rest - middle).astype(BF16).astype(F32)


def stack(rows, height):
    at = iota((height, rows[0].shape[1]), 0)
    out = jnp.zeros(at.shape, F32)
    for place, row in enumerate(rows):
        out = jnp.where(at == place, row, out)
    return out.astype(BF16)


def one_hot(ids, height):
    return jnp.where(iota((height, ids.shape[1]), 0) == ids, 1.0, 0.0).astype(BF16)


def columns(rows, width=LANES):
    return mxu(stack(rows, 8), jnp.ones((8, width), BF16), TN)


def table_rows(table):
    return jnp.concatenate(split3(table), axis=0).astype(BF16)


def look_up(rows, upper, lower_hot, height):
    picked = mxu(rows, lower_hot)
    picked = picked[:height] + picked[height : 2 * height] + picked[2 * height :]
    hit = iota(picked.shape, 0) == upper
    return jnp.sum(jnp.where(hit, picked, 0.0), axis=0, keepdims=True)


def add_up(values, upper, lower_hot, height):
    at = iota((height, values.shape[1]), 0)
    parts = [jnp.where(at == upper, part, 0.0) for part in split3(values)]
    sums = mxu(jnp.concatenate(parts, axis=0).astype(BF16), lower_hot, NT)
    return sums[:height] + sums[height : 2 * height] + sums[2 * height :]


def id_columns(ids):
    upper = ids & ~255
    column = columns([upper.astype(F32), (ids - upper).astype(F32)])
    return jnp.concatenate([column] * (STRATA // LANES), axis=1)


def same_and_later(ids, id_column):
    square = (BLOCK, BLOCK)
    later = iota(square, 1) >= iota(square, 0)
    return jnp.where((id_column == ids.astype(F32)) & later, 1.0, 0.0).astype(BF16)


def members(id_column):
    labels = iota((BLOCK, STRATA), 1).astype(F32)
    return jnp.where(id_column == labels, 1.0, 0.0).astype(BF16)


def strided(start, count):
    return pl.ds(start, count, stride=8)


def weigh_kernel(counts, strata, centers, beta, frailty, covars, w_out, send):
    records = covars.shape[0]
    betas = stack(split3(beta[...]), 8)
    table = table_rows(frailty[...])
    total_zero = jnp.zeros((8, LANES), F32)
    total_one = jnp.zeros((STRATA, LANES), F32)
    for start in range(0, records, BLOCK):
        span = pl.ds(start, BLOCK)
        ids, owners, rows = strata[:, span], centers[:, span], covars[span, :]
        eta = jnp.sum(mxu(betas, rows, NT), axis=0, keepdims=True) + look_up(
            table, owners >> 7, one_hot(owners & 127, LANES), frailty.shape[0]
        )
        live = iota((1, BLOCK), 1) + start < counts[0]
        weight = jnp.where(live, jnp.exp(eta), 0.0)
        w_out[:, span] = weight
        weighted = (columns(split3(weight)) * rows.astype(F32)).astype(BF16)
        total_one = total_one + mxu(one_hot(ids, STRATA), weighted)
        total_zero = total_zero + add_up(weight, ids >> 7, one_hot(ids & 127, LANES), 8)
    devices = send.shape[0]
    send = send.reshape(devices * 8, LANES)
    for place in range(4):
        send[strided(place, devices), :] = jnp.broadcast_to(
            total_zero[place : place + 1], (devices, LANES)
        )
        send[strided(4 + place, devices), :] = total_one[place * LANES : (place + 1) * LANES]


def suffix_kernel(strata, w_in, covars, zero_out, one_out):
    records = covars.shape[0]
    carry_zero = jnp.zeros((8, LANES), F32)
    carry_one = jnp.zeros((STRATA, LANES), F32)
    for start in reversed(range(0, records, BLOCK)):
        span = pl.ds(start, BLOCK)
        ids, weight = strata[:, span], w_in[:, span]
        weighted = (columns(split3(weight)) * covars[span, :].astype(F32)).astype(BF16)
        id_column = id_columns(ids)
        shared = same_and_later(ids, id_column)
        lower_hot = one_hot(ids & 127, LANES)
        zero = jnp.sum(mxu(stack(split3(weight), 8), shared, NT), axis=0, keepdims=True)
        zero_out[:, span] = zero + look_up(table_rows(carry_zero), ids >> 7, lower_hot, 8)
        high = carry_one.astype(BF16)
        low = (carry_one - high.astype(F32)).astype(BF16)
        later = mxu(members(id_column), jnp.concatenate([high, low], axis=1))
        one_out[span, :] = mxu(shared, weighted) + later[:, :LANES] + later[:, LANES:]
        carry_one = carry_one + mxu(one_hot(ids, STRATA), weighted)
        carry_zero = carry_zero + add_up(weight, ids >> 7, lower_hot, 8)


def hazard_kernel(counts, mine, strata, events, zero_in, received, q_out, send, later):
    records = strata.shape[1]
    devices = received.shape[0]
    received = received.reshape(devices * 8, LANES)
    send = send.reshape(devices * 8, LANES)
    running = jnp.zeros((8, LANES), F32)
    for device in reversed(range(devices)):
        slab = pl.ds(device * 8, 8)
        later[slab, :] = running
        running = running + received[slab, :]
    table = table_rows(later[pl.ds(pl.multiple_of(mine[0] * 8, 8), 8), :])
    total = jnp.zeros((8, LANES), F32)
    for start in range(0, records, BLOCK):
        span = pl.ds(start, BLOCK)
        ids = strata[:, span]
        lower_hot = one_hot(ids & 127, LANES)
        zero = zero_in[:, span] + look_up(table, ids >> 7, lower_hot, 8)
        live = iota((1, BLOCK), 1) + start < counts[0]
        happened = live & (events[:, span] > 0)
        increment = jnp.where(happened, 1.0 / jnp.where(happened, zero, 1.0), 0.0)
        q_out[:, span] = increment
        total = total + add_up(increment, ids >> 7, lower_hot, 8)
    mask = iota((8, LANES), 0) < 4
    for device in range(devices):
        slab = pl.ds(device * 8, 8)
        send[slab, :] = jnp.where(mask, total, later[slab, :])


def prefix_kernel(strata, q_in, out):
    records = strata.shape[1]
    carry = jnp.zeros((8, LANES), F32)
    for start in range(0, records, BLOCK):
        span = pl.ds(start, BLOCK)
        ids, increment = strata[:, span], q_in[:, span]
        shared = same_and_later(ids, id_columns(ids))
        lower_hot = one_hot(ids & 127, LANES)
        local = jnp.sum(mxu(stack(split3(increment), 8), shared), axis=0, keepdims=True)
        out[:, span] = local + look_up(table_rows(carry), ids >> 7, lower_hot, 8)
        carry = carry + add_up(increment, ids >> 7, lower_hot, 8)


def moments_kernel(
    counts, mine, strata, centers, events, w_in, q_in, hazard_in, received, covars, one_in,
    loaded_out, pack, low_out,
):
    records, width = covars.shape
    devices = received.shape[0]
    received = received.reshape(devices * 8, LANES)
    before = (iota((devices * 8, LANES), 0) >> 3) < mine[0]
    earlier = jnp.where(before, received[...], 0.0).reshape(devices, 8, LANES).sum(axis=0)
    table = table_rows(earlier)
    later = jnp.concatenate([received[strided(4 + r, devices), :] for r in range(4)], axis=0)
    high = later.astype(BF16)
    low = (later - high.astype(F32)).astype(BF16)
    later = jnp.concatenate([high, low], axis=1)
    sixteen = iota((16, 3 * LANES), 0)
    group = iota((16, 3 * LANES), 1) >> 7
    spread = jnp.where(
        (sixteen < 8) & (group == jnp.where(sixteen < 3, 0, jnp.where(sixteen < 6, 1, 2))), 1.0, 0.0
    ).astype(BF16)
    groups = 16
    pairs = jnp.zeros((4 * groups, LANES), F32)
    curvature = jnp.zeros((width, width), F32)
    gradient = jnp.zeros((1, width), F32)
    for start in range(0, records, BLOCK):
        span = pl.ds(start, BLOCK)
        ids, owners, rows = strata[:, span], centers[:, span], covars[span, :]
        increment = q_in[:, span]
        hazard = hazard_in[:, span] + look_up(table, ids >> 7, one_hot(ids & 127, LANES), 8)
        exposure = w_in[:, span] * hazard
        live = iota((1, BLOCK), 1) + start < counts[0]
        happened = jnp.where(live & (events[:, span] > 0), 1.0, 0.0)
        parts = split3(exposure)
        top = ids & ~255
        both = mxu(stack([*parts, *split3(increment), top.astype(F32), (ids - top).astype(F32)], 16), spread, TN)
        loaded = (both[:, :LANES] * rows.astype(F32)).astype(BF16)
        loaded_out[span, :] = loaded
        outside = mxu(members(jnp.concatenate([both[:, 2 * LANES :]] * 4, axis=1)), later)
        mean = (one_in[span, :] + outside[:, :LANES] + outside[:, LANES:]) * both[:, LANES : 2 * LANES]
        mean_low = mean.astype(BF16)
        low_out[span, :] = mean_low
        flags = mxu(stack([happened], 8), rows)
        gradient = gradient + flags[:1] - jnp.sum(mean, axis=0, keepdims=True)
        at = iota((groups, BLOCK), 0)
        chosen = [jnp.where(at == owners >> 7, part, 0.0) for part in (*parts, happened)]
        pairs = pairs + mxu(
            jnp.concatenate(chosen, axis=0).astype(BF16), one_hot(owners & 127, LANES), NT
        )
    curvature = mxu(covars[...], loaded_out[...], TN) - mxu(low_out[...], low_out[...], TN)
    exposed = pairs[:groups] + pairs[groups : 2 * groups] + pairs[2 * groups : 3 * groups]
    pack[0:width, :] = curvature
    pack[width : width + 8, :] = jnp.broadcast_to(gradient, (8, width))
    pack[width + 8 : width + 24, :] = pairs[3 * groups :] - exposed
    pack[width + 24 : width + 40, :] = exposed


def cross_kernel(centers, loaded, core_zero, core_one):
    records, width = loaded.shape
    groups = 8
    ids = centers[...]
    within = ids & 255
    upper = jnp.concatenate(
        [columns([(ids[:, at : at + BLOCK] >> 8).astype(F32)]) for at in range(0, records, BLOCK)],
        axis=0,
    ).astype(BF16)
    rows = loaded[...]
    chosen = jnp.concatenate(
        [jnp.where(upper == group, rows, jnp.zeros_like(rows)) for group in range(groups)], axis=1
    )
    place = ((within >> 6) & 1) * LANES + (within >> 7) * 64 + (within & 63)
    sums = mxu(one_hot(place, 2 * LANES), chosen)
    for group in range(groups):
        lanes = pl.ds(group * width, width)
        part = sums[:, group * width : (group + 1) * width]
        core_zero[pl.ds(group * LANES, LANES), :] = part[:LANES]
        core_one[pl.ds(group * LANES, LANES), :] = part[LANES:]


def last_kernel(
    load, devices, mine, first, second, third, fourth, shares, frailty,
    info, score, center_score, center_info, center_cross,
):
    width = info.shape[0]
    pack = (first[...] + third[...]) + (second[...] + fourth[...])
    total = load * CENTERS_DEV * devices
    root = math.sqrt(load)
    info[...] = pack[:width] / total
    score[...] = pack[width : width + 1] / math.sqrt(total)
    hit = iota((16, LANES), 0) == mine[0] >> 3
    turn = (LANES - (mine[0] & 7) * CENTERS_DEV) & (LANES - 1)

    def own(table):
        row = jnp.sum(jnp.where(hit, table, 0.0), axis=0, keepdims=True)
        return pltpu.roll(jnp.broadcast_to(row, (8, LANES)), turn, 1)[:1]

    own_score = own(pack[width + 8 : width + 24]) / root - 0.5 * own(frailty[...])
    own_info = own(pack[width + 24 :]) / load + 0.5
    center_score[...] = own_score[:, :CENTERS_DEV]
    center_info[...] = own_info[:, :CENTERS_DEV]
    center_cross[...] = jnp.sum(shares[...], axis=0) / root


def call(kernel, out_shape, scratch=(), scalars=0, near=True):
    def run(*args):
        arrays = len(args) - scalars
        spaces = [pltpu.SMEM] * scalars + [pltpu.VMEM] * arrays
        place = pltpu.VMEM if near else pltpu.HBM
        return pl.pallas_call(
            kernel,
            out_shape=out_shape,
            in_specs=[pl.BlockSpec(memory_space=space) for space in spaces],
            out_specs=jax.tree.map(lambda _: pl.BlockSpec(memory_space=pltpu.VMEM), out_shape),
            scratch_shapes=list(scratch),
            compiler_params=pltpu.CompilerParams(vmem_limit_bytes=12 * 2**20),
        )(
            *args[:scalars],
            *(pltpu.with_memory_space_constraint(arg, place) for arg in args[scalars:]),
        )

    return run


def shaped(*shape, dtype=F32):
    return pltpu.VMEM(shape, dtype)


def place_of(z, y, c, x):
    return ((z * 4 + y) * 2 + c) * 4 + x


def moves(step):
    grid = [
        (z, y, c, x) for z in range(4) for y in range(4) for c in range(2) for x in range(4)
    ]
    return [(place_of(*at), place_of(*step(*at))) for at in grid]


def gather_ring(value, name):
    axis = "zyx".index(name)

    def ahead(k):
        def step(z, y, c, x):
            at = [z, y, x]
            at[axis] = (at[axis] + k) % 4
            return at[0], at[1], c, at[2]

        return step

    return [value] + [lax.ppermute(value, AXES, moves(ahead(k))) for k in (1, 2, 3)]


def sum_ring(value, name):
    here, one, two, three = gather_ring(value, name)
    return (here + two) + (one + three)


def other_core(value):
    return lax.ppermute(value, AXES, moves(lambda z, y, c, x: (z, y, 1 - c, x)))


def exchange(value, axes=AXES):
    return lax.all_to_all(value, axes, 0, 0, tiled=True)


def body(covars, strata, centers, events, counts, beta, frailty):
    records, width = covars.shape
    devices = math.prod(lax.axis_size(axis) for axis in AXES)
    center_total = CENTERS_DEV * devices
    mine = lax.axis_index(AXES)
    me = mine.reshape(1).astype(jnp.int32)
    strata, centers, events = (part.reshape(1, records) for part in (strata, centers, events))
    slabs = shaped(devices, 8, LANES)
    line = shaped(1, records)
    weights, totals = call(weigh_kernel, (line, slabs), scalars=1, near=False)(
        counts, strata, centers, beta.reshape(1, width), frailty.reshape(-1, LANES), covars
    )
    received = exchange(totals)
    suffix_zero, suffix_one = call(suffix_kernel, (line, shaped(records, width)))(
        strata, weights, covars
    )
    increments, send = call(
        hazard_kernel, (line, slabs), scratch=[pltpu.VMEM((devices * 8, LANES), F32)], scalars=2
    )(counts, me, strata, events, suffix_zero, received)
    arrived = exchange(send)
    local_hazard = call(prefix_kernel, line)(strata, increments)
    loaded, pack = call(
        moments_kernel,
        (pltpu.HBM((records, width), BF16), shaped(width + 40, LANES)),
        scratch=[pltpu.VMEM((records, width), BF16)],
        scalars=2,
    )(
        counts, me, strata, centers, events, weights, increments, local_hazard, arrived,
        covars, suffix_one,
    )
    swapped = other_core(pack)
    half = shaped(center_total // 2, width)
    core_zero, core_one = call(cross_kernel, (half, half), near=False)(centers, loaded)
    pack = sum_ring(pack + swapped, "x")
    is_one = lax.axis_index("core") == 1
    keep = jnp.where(is_one, core_one, core_zero)
    give = jnp.where(is_one, core_zero, core_one)
    cross = keep + other_core(give)
    shares = exchange(cross.reshape(devices // 2, CENTERS_DEV, width), CHIPS)
    pack = sum_ring(pack, "y")
    parts = gather_ring(pack, "z")
    last = call(
        functools.partial(last_kernel, records // CENTERS_DEV, devices),
        (
            jax.ShapeDtypeStruct((width, width), F32),
            jax.ShapeDtypeStruct((1, width), F32),
            jax.ShapeDtypeStruct((1, CENTERS_DEV), F32),
            jax.ShapeDtypeStruct((1, CENTERS_DEV), F32),
            jax.ShapeDtypeStruct((CENTERS_DEV, width), F32),
        ),
        scalars=1,
    )
    info, score, center_score, center_info, center_cross = last(
        me, *parts, shares, frailty.reshape(-1, LANES)
    )
    return (
        score.reshape(width),
        info,
        center_score.reshape(CENTERS_DEV),
        center_info.reshape(CENTERS_DEV),
        center_cross,
    )


def solution(mesh):
    mesh = Mesh(mesh.devices.reshape(4, 4, 2, 4), AXES)
    in_specs = (
        P(AXES, None),
        P(AXES),
        P(AXES),
        P(AXES),
        P(AXES),
        P(),
        P(),
    )
    out_specs = (P(), P(), P(AXES), P(AXES), P(AXES, None))
    return jax.shard_map(body, mesh=mesh, in_specs=in_specs, out_specs=out_specs, check_vma=False)
```

```python
import functools
import math

import jax
import jax.numpy as jnp
from jax import lax
from jax.experimental import pallas as pl
from jax.experimental.pallas import tpu as pltpu
from jax.sharding import Mesh
from jax.sharding import PartitionSpec as P


STRATA = 512
CENTERS_DEV = 16
AXES = ("z", "y", "core", "x")
CHIPS = ("z", "y", "x")
BLOCK = 512
WIDE = 1024
LANES = 128
F32 = jnp.float32
BF16 = jnp.bfloat16
NN = (((1,), (0,)), ((), ()))
NT = (((1,), (1,)), ((), ()))
TN = (((0,), (0,)), ((), ()))


def mxu(left, right, dims=NN):
    return lax.dot_general(left, right, dims, preferred_element_type=F32)


def iota(shape, dim):
    return lax.broadcasted_iota(jnp.int32, shape, dim)


def split3(value):
    high = value.astype(BF16).astype(F32)
    rest = value - high
    middle = rest.astype(BF16).astype(F32)
    return high, middle, (rest - middle).astype(BF16).astype(F32)


def stack(rows, height):
    at = iota((height, rows[0].shape[1]), 0)
    out = jnp.zeros(at.shape, F32)
    for place, row in enumerate(rows):
        out = jnp.where(at == place, row, out)
    return out.astype(BF16)


def one_hot(ids, height):
    return jnp.where(iota((height, ids.shape[1]), 0) == ids, 1.0, 0.0).astype(BF16)


def columns(rows, width=LANES):
    return mxu(stack(rows, 8), jnp.ones((8, width), BF16), TN)


def table_rows(table):
    return jnp.concatenate(split3(table), axis=0).astype(BF16)


def look_up(rows, upper, lower_hot, height):
    picked = mxu(rows, lower_hot)
    picked = picked[:height] + picked[height : 2 * height] + picked[2 * height :]
    hit = iota(picked.shape, 0) == upper
    return jnp.sum(jnp.where(hit, picked, 0.0), axis=0, keepdims=True)


def add_up(values, upper, lower_hot, height):
    at = iota((height, values.shape[1]), 0)
    parts = [jnp.where(at == upper, part, 0.0) for part in split3(values)]
    sums = mxu(jnp.concatenate(parts, axis=0).astype(BF16), lower_hot, NT)
    return sums[:height] + sums[height : 2 * height] + sums[2 * height :]


def id_columns(ids):
    upper = ids & ~255
    column = columns([upper.astype(F32), (ids - upper).astype(F32)])
    return jnp.concatenate([column] * (STRATA // LANES), axis=1)


def same_and_later(ids, id_column):
    square = (BLOCK, BLOCK)
    later = iota(square, 1) >= iota(square, 0)
    return jnp.where((id_column == ids.astype(F32)) & later, 1.0, 0.0).astype(BF16)


def members(id_column):
    labels = iota(id_column.shape, 1).astype(F32)
    return jnp.where(id_column == labels, 1.0, 0.0).astype(BF16)


def strided(start, count):
    return pl.ds(start, count, stride=8)


def weigh_kernel(counts, strata, centers, beta, frailty, covars, w_out, send):
    records = covars.shape[0]
    betas = stack(split3(beta[...]), 8)
    table = table_rows(frailty[...])
    total_zero = jnp.zeros((8, LANES), F32)
    total_one = jnp.zeros((STRATA, LANES), F32)
    for start in range(0, records, BLOCK):
        span = pl.ds(start, BLOCK)
        ids, owners, rows = strata[:, span], centers[:, span], covars[span, :]
        eta = jnp.sum(mxu(betas, rows, NT), axis=0, keepdims=True) + look_up(
            table, owners >> 7, one_hot(owners & 127, LANES), frailty.shape[0]
        )
        live = iota((1, BLOCK), 1) + start < counts[0]
        weight = jnp.where(live, jnp.exp(eta), 0.0)
        w_out[:, span] = weight
        weighted = (columns(split3(weight)) * rows.astype(F32)).astype(BF16)
        total_one = total_one + mxu(one_hot(ids, STRATA), weighted)
        total_zero = total_zero + add_up(weight, ids >> 7, one_hot(ids & 127, LANES), 8)
    devices = send.shape[0]
    send = send.reshape(devices * 8, LANES)
    for place in range(4):
        send[strided(place, devices), :] = jnp.broadcast_to(
            total_zero[place : place + 1], (devices, LANES)
        )
        send[strided(4 + place, devices), :] = total_one[place * LANES : (place + 1) * LANES]


def suffix_kernel(strata, w_in, covars, zero_out, one_out):
    records = covars.shape[0]
    carry_zero = jnp.zeros((8, LANES), F32)
    carry_one = jnp.zeros((STRATA, LANES), F32)
    for start in reversed(range(0, records, BLOCK)):
        span = pl.ds(start, BLOCK)
        ids, weight = strata[:, span], w_in[:, span]
        weighted = (columns(split3(weight)) * covars[span, :].astype(F32)).astype(BF16)
        id_column = id_columns(ids)
        shared = same_and_later(ids, id_column)
        lower_hot = one_hot(ids & 127, LANES)
        zero = jnp.sum(mxu(stack(split3(weight), 8), shared, NT), axis=0, keepdims=True)
        zero_out[:, span] = zero + look_up(table_rows(carry_zero), ids >> 7, lower_hot, 8)
        high = carry_one.astype(BF16)
        low = (carry_one - high.astype(F32)).astype(BF16)
        later = mxu(members(id_column), jnp.concatenate([high, low], axis=1))
        one_out[span, :] = mxu(shared, weighted) + later[:, :LANES] + later[:, LANES:]
        carry_one = carry_one + mxu(one_hot(ids, STRATA), weighted)
        carry_zero = carry_zero + add_up(weight, ids >> 7, lower_hot, 8)


def hazard_kernel(counts, mine, strata, events, zero_in, received, q_out, send, later):
    records = strata.shape[1]
    devices = received.shape[0]
    received = received.reshape(devices * 8, LANES)
    send = send.reshape(devices * 8, LANES)
    running = jnp.zeros((8, LANES), F32)
    for device in reversed(range(devices)):
        slab = pl.ds(device * 8, 8)
        later[slab, :] = running
        running = running + received[slab, :]
    table = table_rows(later[pl.ds(pl.multiple_of(mine[0] * 8, 8), 8), :])
    total = jnp.zeros((8, LANES), F32)
    for start in range(0, records, BLOCK):
        span = pl.ds(start, BLOCK)
        ids = strata[:, span]
        lower_hot = one_hot(ids & 127, LANES)
        zero = zero_in[:, span] + look_up(table, ids >> 7, lower_hot, 8)
        live = iota((1, BLOCK), 1) + start < counts[0]
        happened = live & (events[:, span] > 0)
        increment = jnp.where(happened, 1.0 / jnp.where(happened, zero, 1.0), 0.0)
        q_out[:, span] = increment
        total = total + add_up(increment, ids >> 7, lower_hot, 8)
    mask = iota((8, LANES), 0) < 4
    for device in range(devices):
        slab = pl.ds(device * 8, 8)
        send[slab, :] = jnp.where(mask, total, later[slab, :])


def prefix_kernel(strata, q_in, out):
    records = strata.shape[1]
    carry = jnp.zeros((8, LANES), F32)
    for start in range(0, records, BLOCK):
        span = pl.ds(start, BLOCK)
        ids, increment = strata[:, span], q_in[:, span]
        shared = same_and_later(ids, id_columns(ids))
        lower_hot = one_hot(ids & 127, LANES)
        local = jnp.sum(mxu(stack(split3(increment), 8), shared), axis=0, keepdims=True)
        out[:, span] = local + look_up(table_rows(carry), ids >> 7, lower_hot, 8)
        carry = carry + add_up(increment, ids >> 7, lower_hot, 8)


def moments_kernel(
    counts, mine, strata, centers, events, w_in, q_in, hazard_in, received, covars, one_in,
    loaded_out, pack, low_out,
):
    records, width = covars.shape
    devices = received.shape[0]
    received = received.reshape(devices * 8, LANES)
    before = (iota((devices * 8, LANES), 0) >> 3) < mine[0]
    earlier = jnp.where(before, received[...], 0.0).reshape(devices, 8, LANES).sum(axis=0)
    table = table_rows(earlier)
    later = jnp.concatenate([received[strided(4 + r, devices), :] for r in range(4)], axis=0)
    high = later.astype(BF16)
    low = (later - high.astype(F32)).astype(BF16)
    later = jnp.concatenate([high, low], axis=1)
    sixteen = iota((16, 3 * LANES), 0)
    group = iota((16, 3 * LANES), 1) >> 7
    spread = jnp.where(
        (sixteen < 8) & (group == jnp.where(sixteen < 3, 0, jnp.where(sixteen < 6, 1, 2))), 1.0, 0.0
    ).astype(BF16)
    groups = 16
    pairs = jnp.zeros((4 * groups, LANES), F32)
    curvature = jnp.zeros((width, width), F32)
    gradient = jnp.zeros((1, width), F32)
    for start in range(0, records, WIDE):
        span = pl.ds(start, WIDE)
        ids, owners, rows = strata[:, span], centers[:, span], covars[span, :]
        increment = q_in[:, span]
        hazard = hazard_in[:, span] + look_up(table, ids >> 7, one_hot(ids & 127, LANES), 8)
        exposure = w_in[:, span] * hazard
        live = iota((1, WIDE), 1) + start < counts[0]
        happened = jnp.where(live & (events[:, span] > 0), 1.0, 0.0)
        parts = split3(exposure)
        top = ids & ~255
        both = mxu(stack([*parts, *split3(increment), top.astype(F32), (ids - top).astype(F32)], 16), spread, TN)
        loaded = (both[:, :LANES] * rows.astype(F32)).astype(BF16)
        loaded_out[span, :] = loaded
        outside = mxu(members(jnp.concatenate([both[:, 2 * LANES :]] * 4, axis=1)), later)
        mean = (one_in[span, :] + outside[:, :LANES] + outside[:, LANES:]) * both[:, LANES : 2 * LANES]
        mean_low = mean.astype(BF16)
        low_out[span, :] = mean_low
        flags = mxu(stack([happened], 8), rows)
        gradient = gradient + flags[:1] - jnp.sum(mean, axis=0, keepdims=True)
        at = iota((groups, WIDE), 0)
        chosen = [jnp.where(at == owners >> 7, part, 0.0) for part in (*parts, happened)]
        pairs = pairs + mxu(
            jnp.concatenate(chosen, axis=0).astype(BF16), one_hot(owners & 127, LANES), NT
        )
    curvature = mxu(covars[...], loaded_out[...], TN) - mxu(low_out[...], low_out[...], TN)
    exposed = pairs[:groups] + pairs[groups : 2 * groups] + pairs[2 * groups : 3 * groups]
    pack[0:width, :] = curvature
    pack[width : width + 8, :] = jnp.broadcast_to(gradient, (8, width))
    pack[width + 8 : width + 24, :] = pairs[3 * groups :] - exposed
    pack[width + 24 : width + 40, :] = exposed


def cross_kernel(centers, loaded, core_zero, core_one):
    records, width = loaded.shape
    groups = 8
    ids = centers[...]
    within = ids & 255
    upper = jnp.concatenate(
        [columns([(ids[:, at : at + BLOCK] >> 8).astype(F32)]) for at in range(0, records, BLOCK)],
        axis=0,
    ).astype(BF16)
    rows = loaded[...]
    chosen = jnp.concatenate(
        [jnp.where(upper == group, rows, jnp.zeros_like(rows)) for group in range(groups)], axis=1
    )
    place = ((within >> 6) & 1) * LANES + (within >> 7) * 64 + (within & 63)
    sums = mxu(one_hot(place, 2 * LANES), chosen)
    for group in range(groups):
        lanes = pl.ds(group * width, width)
        part = sums[:, group * width : (group + 1) * width]
        core_zero[pl.ds(group * LANES, LANES), :] = part[:LANES]
        core_one[pl.ds(group * LANES, LANES), :] = part[LANES:]


def last_kernel(
    load, devices, mine, first, second, shares, frailty,
    info, score, center_score, center_info, center_cross,
):
    width = info.shape[0]
    pack = first[...] + second[...]
    total = load * CENTERS_DEV * devices
    root = math.sqrt(load)
    info[...] = pack[:width] / total
    score[...] = pack[width : width + 1] / math.sqrt(total)
    hit = iota((16, LANES), 0) == mine[0] >> 3
    turn = (LANES - (mine[0] & 7) * CENTERS_DEV) & (LANES - 1)

    def own(table):
        row = jnp.sum(jnp.where(hit, table, 0.0), axis=0, keepdims=True)
        return pltpu.roll(jnp.broadcast_to(row, (8, LANES)), turn, 1)[:1]

    own_score = own(pack[width + 8 : width + 24]) / root - 0.5 * own(frailty[...])
    own_info = own(pack[width + 24 :]) / load + 0.5
    center_score[...] = own_score[:, :CENTERS_DEV]
    center_info[...] = own_info[:, :CENTERS_DEV]
    center_cross[...] = jnp.sum(shares[...], axis=0) / root


def call(kernel, out_shape, scratch=(), scalars=0, near=True):
    def run(*args):
        arrays = len(args) - scalars
        spaces = [pltpu.SMEM] * scalars + [pltpu.VMEM] * arrays
        place = pltpu.VMEM if near else pltpu.HBM
        return pl.pallas_call(
            kernel,
            out_shape=out_shape,
            in_specs=[pl.BlockSpec(memory_space=space) for space in spaces],
            out_specs=jax.tree.map(lambda _: pl.BlockSpec(memory_space=pltpu.VMEM), out_shape),
            scratch_shapes=list(scratch),
            compiler_params=pltpu.CompilerParams(vmem_limit_bytes=12 * 2**20),
        )(
            *args[:scalars],
            *(pltpu.with_memory_space_constraint(arg, place) for arg in args[scalars:]),
        )

    return run


def shaped(*shape, dtype=F32):
    return pltpu.VMEM(shape, dtype)


def place_of(z, y, c, x):
    return ((z * 4 + y) * 2 + c) * 4 + x


def moves(step):
    grid = [
        (z, y, c, x) for z in range(4) for y in range(4) for c in range(2) for x in range(4)
    ]
    return [(place_of(*at), place_of(*step(*at))) for at in grid]


def gather_ring(value, name):
    axis = "zyx".index(name)

    def ahead(k):
        def step(z, y, c, x):
            at = [z, y, x]
            at[axis] = (at[axis] + k) % 4
            return at[0], at[1], c, at[2]

        return step

    return [value] + [lax.ppermute(value, AXES, moves(ahead(k))) for k in (1, 2, 3)]


def sum_ring(value, name):
    here, one, two, three = gather_ring(value, name)
    return (here + two) + (one + three)


def other_core(value):
    return lax.ppermute(value, AXES, moves(lambda z, y, c, x: (z, y, 1 - c, x)))


def exchange(value, axes=AXES):
    return lax.all_to_all(value, axes, 0, 0, tiled=True)


def body(covars, strata, centers, events, counts, beta, frailty):
    records, width = covars.shape
    devices = math.prod(lax.axis_size(axis) for axis in AXES)
    center_total = CENTERS_DEV * devices
    mine = lax.axis_index(AXES)
    me = mine.reshape(1).astype(jnp.int32)
    strata, centers, events = (part.reshape(1, records) for part in (strata, centers, events))
    slabs = shaped(devices, 8, LANES)
    line = shaped(1, records)
    weights, totals = call(weigh_kernel, (line, slabs), scalars=1, near=False)(
        counts, strata, centers, beta.reshape(1, width), frailty.reshape(-1, LANES), covars
    )
    received = exchange(totals)
    suffix_zero, suffix_one = call(suffix_kernel, (line, shaped(records, width)))(
        strata, weights, covars
    )
    increments, send = call(
        hazard_kernel, (line, slabs), scratch=[pltpu.VMEM((devices * 8, LANES), F32)], scalars=2
    )(counts, me, strata, events, suffix_zero, received)
    arrived = exchange(send)
    local_hazard = call(prefix_kernel, line)(strata, increments)
    loaded, pack = call(
        moments_kernel,
        (pltpu.HBM((records, width), BF16), shaped(width + 40, LANES)),
        scratch=[pltpu.VMEM((records, width), BF16)],
        scalars=2,
    )(
        counts, me, strata, centers, events, weights, increments, local_hazard, arrived,
        covars, suffix_one,
    )
    swapped = other_core(pack)
    half = shaped(center_total // 2, width)
    core_zero, core_one = call(cross_kernel, (half, half), near=False)(centers, loaded)
    pack = sum_ring(pack + swapped, "z")
    is_one = lax.axis_index("core") == 1
    keep = jnp.where(is_one, core_one, core_zero)
    give = jnp.where(is_one, core_zero, core_one)
    cross = keep + other_core(give)
    shares = exchange(cross.reshape(devices // 2, CENTERS_DEV, width), CHIPS)
    pack = sum_ring(pack, "y")
    pack = pack + lax.ppermute(pack, AXES, moves(lambda z, y, c, x: (z, y, c, x ^ 1)))
    other = lax.ppermute(pack, AXES, moves(lambda z, y, c, x: (z, y, c, x ^ 3)))
    parts = [pack, other]
    last = call(
        functools.partial(last_kernel, records // CENTERS_DEV, devices),
        (
            jax.ShapeDtypeStruct((width, width), F32),
            jax.ShapeDtypeStruct((1, width), F32),
            jax.ShapeDtypeStruct((1, CENTERS_DEV), F32),
            jax.ShapeDtypeStruct((1, CENTERS_DEV), F32),
            jax.ShapeDtypeStruct((CENTERS_DEV, width), F32),
        ),
        scalars=1,
    )
    info, score, center_score, center_info, center_cross = last(
        me, *parts, shares, frailty.reshape(-1, LANES)
    )
    return (
        score.reshape(width),
        info,
        center_score.reshape(CENTERS_DEV),
        center_info.reshape(CENTERS_DEV),
        center_cross,
    )


def solution(mesh):
    mesh = Mesh(mesh.devices.reshape(4, 4, 2, 4), AXES)
    in_specs = (
        P(AXES, None),
        P(AXES),
        P(AXES),
        P(AXES),
        P(AXES),
        P(),
        P(),
    )
    out_specs = (P(), P(), P(AXES), P(AXES), P(AXES, None))
    return jax.shard_map(body, mesh=mesh, in_specs=in_specs, out_specs=out_specs, check_vma=False)
```

```python
import functools
import math

import jax
import jax.numpy as jnp
from jax import lax
from jax.experimental import pallas as pl
from jax.experimental.pallas import tpu as pltpu
from jax.sharding import Mesh
from jax.sharding import PartitionSpec as P


STRATA = 512
CENTERS_DEV = 16
AXES = ("z", "y", "core", "x")
CHIPS = ("z", "y", "x")
BLOCK = 512
WIDE = 1024
ALL = 4096
LANES = 128
F32 = jnp.float32
BF16 = jnp.bfloat16
NN = (((1,), (0,)), ((), ()))
NT = (((1,), (1,)), ((), ()))
TN = (((0,), (0,)), ((), ()))


def mxu(left, right, dims=NN):
    return lax.dot_general(left, right, dims, preferred_element_type=F32)


def iota(shape, dim):
    return lax.broadcasted_iota(jnp.int32, shape, dim)


def split3(value):
    high = value.astype(BF16).astype(F32)
    rest = value - high
    middle = rest.astype(BF16).astype(F32)
    return high, middle, (rest - middle).astype(BF16).astype(F32)


def stack(rows, height):
    at = iota((height, rows[0].shape[1]), 0)
    out = jnp.zeros(at.shape, F32)
    for place, row in enumerate(rows):
        out = jnp.where(at == place, row, out)
    return out.astype(BF16)


def one_hot(ids, height):
    return jnp.where(iota((height, ids.shape[1]), 0) == ids, 1.0, 0.0).astype(BF16)


def columns(rows, width=LANES):
    return mxu(stack(rows, 8), jnp.ones((8, width), BF16), TN)


def table_rows(table):
    return jnp.concatenate(split3(table), axis=0).astype(BF16)


def look_up(rows, upper, lower_hot, height):
    picked = mxu(rows, lower_hot)
    picked = picked[:height] + picked[height : 2 * height] + picked[2 * height :]
    hit = iota(picked.shape, 0) == upper
    return jnp.sum(jnp.where(hit, picked, 0.0), axis=0, keepdims=True)


def add_up(values, upper, lower_hot, height):
    at = iota((height, values.shape[1]), 0)
    parts = [jnp.where(at == upper, part, 0.0) for part in split3(values)]
    sums = mxu(jnp.concatenate(parts, axis=0).astype(BF16), lower_hot, NT)
    return sums[:height] + sums[height : 2 * height] + sums[2 * height :]


def id_columns(ids):
    upper = ids & ~255
    column = columns([upper.astype(F32), (ids - upper).astype(F32)])
    return jnp.concatenate([column] * (STRATA // LANES), axis=1)


def same_and_later(ids, id_column):
    square = (BLOCK, BLOCK)
    later = iota(square, 1) >= iota(square, 0)
    return jnp.where((id_column == ids.astype(F32)) & later, 1.0, 0.0).astype(BF16)


def members(id_column):
    labels = iota(id_column.shape, 1).astype(F32)
    return jnp.where(id_column == labels, 1.0, 0.0).astype(BF16)


def strided(start, count):
    return pl.ds(start, count, stride=8)


def weigh_kernel(counts, strata, centers, beta, frailty, covars, w_out, send):
    records = covars.shape[0]
    betas = stack(split3(beta[...]), 8)
    table = table_rows(frailty[...])
    total_zero = jnp.zeros((8, LANES), F32)
    total_one = jnp.zeros((STRATA, LANES), F32)
    for start in range(0, records, WIDE):
        span = pl.ds(start, WIDE)
        ids, owners, rows = strata[:, span], centers[:, span], covars[span, :]
        eta = jnp.sum(mxu(betas, rows, NT), axis=0, keepdims=True) + look_up(
            table, owners >> 7, one_hot(owners & 127, LANES), frailty.shape[0]
        )
        live = iota((1, WIDE), 1) + start < counts[0]
        weight = jnp.where(live, jnp.exp(eta), 0.0)
        w_out[:, span] = weight
        weighted = (columns(split3(weight)) * rows.astype(F32)).astype(BF16)
        total_one = total_one + mxu(one_hot(ids, STRATA), weighted)
        total_zero = total_zero + add_up(weight, ids >> 7, one_hot(ids & 127, LANES), 8)
    devices = send.shape[0]
    send = send.reshape(devices * 8, LANES)
    for place in range(4):
        send[strided(place, devices), :] = jnp.broadcast_to(
            total_zero[place : place + 1], (devices, LANES)
        )
        send[strided(4 + place, devices), :] = total_one[place * LANES : (place + 1) * LANES]


def suffix_kernel(strata, w_in, covars, zero_out, one_out):
    records = covars.shape[0]
    carry_zero = jnp.zeros((8, LANES), F32)
    carry_one = jnp.zeros((STRATA, LANES), F32)
    for start in reversed(range(0, records, BLOCK)):
        span = pl.ds(start, BLOCK)
        ids, weight = strata[:, span], w_in[:, span]
        weighted = (columns(split3(weight)) * covars[span, :].astype(F32)).astype(BF16)
        id_column = id_columns(ids)
        shared = same_and_later(ids, id_column)
        lower_hot = one_hot(ids & 127, LANES)
        zero = jnp.sum(mxu(stack(split3(weight), 8), shared, NT), axis=0, keepdims=True)
        zero_out[:, span] = zero + look_up(table_rows(carry_zero), ids >> 7, lower_hot, 8)
        high = carry_one.astype(BF16)
        low = (carry_one - high.astype(F32)).astype(BF16)
        later = mxu(members(id_column), jnp.concatenate([high, low], axis=1))
        one_out[span, :] = mxu(shared, weighted) + later[:, :LANES] + later[:, LANES:]
        carry_one = carry_one + mxu(one_hot(ids, STRATA), weighted)
        carry_zero = carry_zero + add_up(weight, ids >> 7, lower_hot, 8)


def hazard_kernel(counts, mine, strata, events, zero_in, received, q_out, send, later):
    records = strata.shape[1]
    devices = received.shape[0]
    received = received.reshape(devices * 8, LANES)
    send = send.reshape(devices * 8, LANES)
    running = jnp.zeros((8, LANES), F32)
    for device in reversed(range(devices)):
        slab = pl.ds(device * 8, 8)
        later[slab, :] = running
        running = running + received[slab, :]
    table = table_rows(later[pl.ds(pl.multiple_of(mine[0] * 8, 8), 8), :])
    total = jnp.zeros((8, LANES), F32)
    for start in range(0, records, ALL):
        span = pl.ds(start, ALL)
        ids = strata[:, span]
        lower_hot = one_hot(ids & 127, LANES)
        zero = zero_in[:, span] + look_up(table, ids >> 7, lower_hot, 8)
        live = iota((1, ALL), 1) + start < counts[0]
        happened = live & (events[:, span] > 0)
        increment = jnp.where(happened, 1.0 / jnp.where(happened, zero, 1.0), 0.0)
        q_out[:, span] = increment
        total = total + add_up(increment, ids >> 7, lower_hot, 8)
    mask = iota((8, LANES), 0) < 4
    for device in range(devices):
        slab = pl.ds(device * 8, 8)
        send[slab, :] = jnp.where(mask, total, later[slab, :])


def prefix_kernel(strata, q_in, out):
    records = strata.shape[1]
    carry = jnp.zeros((8, LANES), F32)
    for start in range(0, records, BLOCK):
        span = pl.ds(start, BLOCK)
        ids, increment = strata[:, span], q_in[:, span]
        shared = same_and_later(ids, id_columns(ids))
        lower_hot = one_hot(ids & 127, LANES)
        local = jnp.sum(mxu(stack(split3(increment), 8), shared), axis=0, keepdims=True)
        out[:, span] = local + look_up(table_rows(carry), ids >> 7, lower_hot, 8)
        carry = carry + add_up(increment, ids >> 7, lower_hot, 8)


def moments_kernel(
    counts, mine, strata, centers, events, w_in, q_in, hazard_in, received, covars, one_in,
    loaded_out, pack, low_out,
):
    records, width = covars.shape
    devices = received.shape[0]
    received = received.reshape(devices * 8, LANES)
    before = (iota((devices * 8, LANES), 0) >> 3) < mine[0]
    earlier = jnp.where(before, received[...], 0.0).reshape(devices, 8, LANES).sum(axis=0)
    table = table_rows(earlier)
    later = jnp.concatenate([received[strided(4 + r, devices), :] for r in range(4)], axis=0)
    high = later.astype(BF16)
    low = (later - high.astype(F32)).astype(BF16)
    later = jnp.concatenate([high, low], axis=1)
    sixteen = iota((16, 3 * LANES), 0)
    group = iota((16, 3 * LANES), 1) >> 7
    spread = jnp.where(
        (sixteen < 8) & (group == jnp.where(sixteen < 3, 0, jnp.where(sixteen < 6, 1, 2))), 1.0, 0.0
    ).astype(BF16)
    groups = 16
    pairs = jnp.zeros((4 * groups, LANES), F32)
    curvature = jnp.zeros((width, width), F32)
    gradient = jnp.zeros((1, width), F32)
    for start in range(0, records, WIDE):
        span = pl.ds(start, WIDE)
        ids, owners, rows = strata[:, span], centers[:, span], covars[span, :]
        increment = q_in[:, span]
        hazard = hazard_in[:, span] + look_up(table, ids >> 7, one_hot(ids & 127, LANES), 8)
        exposure = w_in[:, span] * hazard
        live = iota((1, WIDE), 1) + start < counts[0]
        happened = jnp.where(live & (events[:, span] > 0), 1.0, 0.0)
        parts = split3(exposure)
        top = ids & ~255
        both = mxu(stack([*parts, *split3(increment), top.astype(F32), (ids - top).astype(F32)], 16), spread, TN)
        loaded = (both[:, :LANES] * rows.astype(F32)).astype(BF16)
        loaded_out[span, :] = loaded
        outside = mxu(members(jnp.concatenate([both[:, 2 * LANES :]] * 4, axis=1)), later)
        mean = (one_in[span, :] + outside[:, :LANES] + outside[:, LANES:]) * both[:, LANES : 2 * LANES]
        mean_low = mean.astype(BF16)
        low_out[span, :] = mean_low
        flags = mxu(stack([happened], 8), rows)
        gradient = gradient + flags[:1] - jnp.sum(mean, axis=0, keepdims=True)
        at = iota((groups, WIDE), 0)
        chosen = [jnp.where(at == owners >> 7, part, 0.0) for part in (*parts, happened)]
        pairs = pairs + mxu(
            jnp.concatenate(chosen, axis=0).astype(BF16), one_hot(owners & 127, LANES), NT
        )
    curvature = mxu(covars[...], loaded_out[...], TN) - mxu(low_out[...], low_out[...], TN)
    exposed = pairs[:groups] + pairs[groups : 2 * groups] + pairs[2 * groups : 3 * groups]
    pack[0:width, :] = curvature
    pack[width : width + 8, :] = jnp.broadcast_to(gradient, (8, width))
    pack[width + 8 : width + 24, :] = pairs[3 * groups :] - exposed
    pack[width + 24 : width + 40, :] = exposed


def cross_kernel(centers, loaded, core_zero, core_one):
    records, width = loaded.shape
    groups = 8
    ids = centers[...]
    within = ids & 255
    upper = jnp.concatenate(
        [columns([(ids[:, at : at + BLOCK] >> 8).astype(F32)]) for at in range(0, records, BLOCK)],
        axis=0,
    ).astype(BF16)
    rows = loaded[...]
    chosen = jnp.concatenate(
        [jnp.where(upper == group, rows, jnp.zeros_like(rows)) for group in range(groups)], axis=1
    )
    place = ((within >> 6) & 1) * LANES + (within >> 7) * 64 + (within & 63)
    sums = mxu(one_hot(place, 2 * LANES), chosen)
    for group in range(groups):
        lanes = pl.ds(group * width, width)
        part = sums[:, group * width : (group + 1) * width]
        core_zero[pl.ds(group * LANES, LANES), :] = part[:LANES]
        core_one[pl.ds(group * LANES, LANES), :] = part[LANES:]


def last_kernel(
    load, devices, mine, first, second, shares, frailty,
    info, score, center_score, center_info, center_cross,
):
    width = info.shape[0]
    pack = first[...] + second[...]
    total = load * CENTERS_DEV * devices
    root = math.sqrt(load)
    info[...] = pack[:width] / total
    score[...] = pack[width : width + 1] / math.sqrt(total)
    hit = iota((16, LANES), 0) == mine[0] >> 3
    turn = (LANES - (mine[0] & 7) * CENTERS_DEV) & (LANES - 1)

    def own(table):
        row = jnp.sum(jnp.where(hit, table, 0.0), axis=0, keepdims=True)
        return pltpu.roll(jnp.broadcast_to(row, (8, LANES)), turn, 1)[:1]

    own_score = own(pack[width + 8 : width + 24]) / root - 0.5 * own(frailty[...])
    own_info = own(pack[width + 24 :]) / load + 0.5
    center_score[...] = own_score[:, :CENTERS_DEV]
    center_info[...] = own_info[:, :CENTERS_DEV]
    center_cross[...] = jnp.sum(shares[...], axis=0) / root


def call(kernel, out_shape, scratch=(), scalars=0, near=True):
    def run(*args):
        arrays = len(args) - scalars
        spaces = [pltpu.SMEM] * scalars + [pltpu.VMEM] * arrays
        place = pltpu.VMEM if near else pltpu.HBM
        return pl.pallas_call(
            kernel,
            out_shape=out_shape,
            in_specs=[pl.BlockSpec(memory_space=space) for space in spaces],
            out_specs=jax.tree.map(lambda _: pl.BlockSpec(memory_space=pltpu.VMEM), out_shape),
            scratch_shapes=list(scratch),
            compiler_params=pltpu.CompilerParams(vmem_limit_bytes=12 * 2**20),
        )(
            *args[:scalars],
            *(pltpu.with_memory_space_constraint(arg, place) for arg in args[scalars:]),
        )

    return run


def shaped(*shape, dtype=F32):
    return pltpu.VMEM(shape, dtype)


def place_of(z, y, c, x):
    return ((z * 4 + y) * 2 + c) * 4 + x


def moves(step):
    grid = [
        (z, y, c, x) for z in range(4) for y in range(4) for c in range(2) for x in range(4)
    ]
    return [(place_of(*at), place_of(*step(*at))) for at in grid]


def gather_ring(value, name):
    axis = "zyx".index(name)

    def ahead(k):
        def step(z, y, c, x):
            at = [z, y, x]
            at[axis] = (at[axis] + k) % 4
            return at[0], at[1], c, at[2]

        return step

    return [value] + [lax.ppermute(value, AXES, moves(ahead(k))) for k in (1, 2, 3)]


def sum_ring(value, name):
    here, one, two, three = gather_ring(value, name)
    return (here + two) + (one + three)


def other_core(value):
    return lax.ppermute(value, AXES, moves(lambda z, y, c, x: (z, y, 1 - c, x)))


def exchange(value, axes=AXES):
    return lax.all_to_all(value, axes, 0, 0, tiled=True)


def body(covars, strata, centers, events, counts, beta, frailty):
    records, width = covars.shape
    devices = math.prod(lax.axis_size(axis) for axis in AXES)
    center_total = CENTERS_DEV * devices
    mine = lax.axis_index(AXES)
    me = mine.reshape(1).astype(jnp.int32)
    strata, centers, events = (part.reshape(1, records) for part in (strata, centers, events))
    slabs = shaped(devices, 8, LANES)
    line = shaped(1, records)
    weights, totals = call(weigh_kernel, (line, slabs), scalars=1, near=False)(
        counts, strata, centers, beta.reshape(1, width), frailty.reshape(-1, LANES), covars
    )
    received = exchange(totals)
    suffix_zero, suffix_one = call(suffix_kernel, (line, shaped(records, width)))(
        strata, weights, covars
    )
    increments, send = call(
        hazard_kernel, (line, slabs), scratch=[pltpu.VMEM((devices * 8, LANES), F32)], scalars=2
    )(counts, me, strata, events, suffix_zero, received)
    arrived = exchange(send)
    local_hazard = call(prefix_kernel, line)(strata, increments)
    loaded, pack = call(
        moments_kernel,
        (pltpu.HBM((records, width), BF16), shaped(width + 40, LANES)),
        scratch=[pltpu.VMEM((records, width), BF16)],
        scalars=2,
    )(
        counts, me, strata, centers, events, weights, increments, local_hazard, arrived,
        covars, suffix_one,
    )
    swapped = other_core(pack)
    half = shaped(center_total // 2, width)
    core_zero, core_one = call(cross_kernel, (half, half), near=False)(centers, loaded)
    pack = sum_ring(pack + swapped, "z")
    is_one = lax.axis_index("core") == 1
    keep = jnp.where(is_one, core_one, core_zero)
    give = jnp.where(is_one, core_zero, core_one)
    cross = keep + other_core(give)
    shares = exchange(cross.reshape(devices // 2, CENTERS_DEV, width), CHIPS)
    pack = sum_ring(pack, "y")
    pack = pack + lax.ppermute(pack, AXES, moves(lambda z, y, c, x: (z, y, c, x ^ 1)))
    other = lax.ppermute(pack, AXES, moves(lambda z, y, c, x: (z, y, c, x ^ 3)))
    parts = [pack, other]
    last = call(
        functools.partial(last_kernel, records // CENTERS_DEV, devices),
        (
            jax.ShapeDtypeStruct((width, width), F32),
            jax.ShapeDtypeStruct((1, width), F32),
            jax.ShapeDtypeStruct((1, CENTERS_DEV), F32),
            jax.ShapeDtypeStruct((1, CENTERS_DEV), F32),
            jax.ShapeDtypeStruct((CENTERS_DEV, width), F32),
        ),
        scalars=1,
    )
    info, score, center_score, center_info, center_cross = last(
        me, *parts, shares, frailty.reshape(-1, LANES)
    )
    return (
        score.reshape(width),
        info,
        center_score.reshape(CENTERS_DEV),
        center_info.reshape(CENTERS_DEV),
        center_cross,
    )


def solution(mesh):
    mesh = Mesh(mesh.devices.reshape(4, 4, 2, 4), AXES)
    in_specs = (
        P(AXES, None),
        P(AXES),
        P(AXES),
        P(AXES),
        P(AXES),
        P(),
        P(),
    )
    out_specs = (P(), P(), P(AXES), P(AXES), P(AXES, None))
    return jax.shard_map(body, mesh=mesh, in_specs=in_specs, out_specs=out_specs, check_vma=False)
```
